32 devices in a mesh: groups: 2 (over y), seq: 16 (over z, x, core).
Axes of the slice: x: 2, y: 2, z: 4, core: 2. Of those that a mesh axis runs over, the one named last changes fastest.
Arguments:
- queries: bfloat16 [32, 16384], P(('groups', 'seq')), parts along dimension 0, may hold values from -8 to 8
- prompt_keys: bfloat16 [8192, 1024], P(('groups', 'seq')), parts along dimension 0, may hold values from -16 to 16
- prompt_values: bfloat16 [8192, 1024], P(('groups', 'seq')), parts along dimension 0, may hold values from -6 to 6
- suffix_keys: bfloat16 [32, 8, 64, 1024], P(('groups', 'seq')), parts along dimension 0, may hold values from -16 to 16
- suffix_values: bfloat16 [32, 8, 64, 1024], P(('groups', 'seq')), parts along dimension 0, may hold values from -6 to 6
- suffix_lengths: int32 [32], P(('groups', 'seq')), parts along dimension 0, may hold values from 1 to 512, 5120 in all
- block_tables: int32 [32, 8], P(('groups', 'seq')), parts along dimension 0, may hold values from 0 to 7, each once within a row
Outputs:
- attended: bfloat16 [32, 16384], P(('groups', 'seq')), parts along dimension 0
The draws below stay inside these ranges and needn't reach their ends.
There are 2 independent parts, one for each index of `groups`. The reference program is written for one: setup_inputs(seed, part) draws one part's arguments, and reference() takes and returns one part's arrays. A program takes and returns all parts, laid end to end along the dimension named above; each array names one. Nothing has to cross between parts.
Inputs may be any that keep to these rules, and one draw needn't show every extreme that they name: `suffix_lengths`: in each group, one sample has exactly 512 live suffix positions, and the lengths of the group's 16 samples sum to 5120. `block_tables`: each row names every one of the sample's 8 pages once.
All inputs are finite; a program needn't handle non-finite values.
Results may differ from the reference program's by a relative error of at most 0.0025.
Values may be sent and summed in bfloat16 or wider, within the bound.
A program may use at most 64 MiB of HBM per device.

```python
import math
import jax
import jax.numpy as jnp
import numpy as np
from jax import lax

H = 128
KVH = 8
HD = 128
PROMPT_DEV = 256
PAGE = 64
PAGES = 8
PROMPT = 4096
SAMPLES = 16
SUF_MAX = 512
N_SEQ = 16


def base_queries(key):
    queries = 1.5 * jax.random.normal(jax.random.fold_in(key, 11), (SAMPLES, H * HD), jnp.float32)
    return jnp.clip(queries, -8.0, 8.0)


def full_queries(key):
    queries = base_queries(key)
    return queries


def draw_queries(key, part):
    return full_queries(key).astype(jnp.bfloat16)


def draw_prompt_keys(key, part):
    prompt_keys = 2.0 * jax.random.normal(jax.random.fold_in(key, 17), (PROMPT, KVH * HD), jnp.float32)
    return jnp.clip(prompt_keys, -16.0, 16.0).astype(jnp.bfloat16)


def draw_suffix_keys(key, part):
    queries = full_queries(key).reshape(SAMPLES, KVH, H // KVH, HD)
    group_mean = jnp.mean(queries, axis=2).reshape(SAMPLES, 1, 1, KVH * HD)
    noise = jax.random.normal(jax.random.fold_in(key, 23), (SAMPLES, PAGES, PAGE, KVH * HD), jnp.float32)
    suffix_keys = 2.0 * noise + 4.0 * group_mean
    return jnp.clip(suffix_keys, -16.0, 16.0).astype(jnp.bfloat16)


def levels(rng, dims, pieces, low, largest):
    level, own = 1.0, jax.random.fold_in(rng, 6)
    for position, parts in pieces:
        steps = jnp.exp(jax.random.uniform(jax.random.fold_in(own, position), (parts,), jnp.float32, low / len(pieces), largest / len(pieces)))
        level = level * jnp.repeat(steps, dims[position] // parts).reshape([-1 if axis == position else 1 for axis in range(len(dims))])
    return level


def split_up(count, total, most, lean):
    portions = [(1 << 20) // math.isqrt(rank ** lean) + 1 for rank in range(2, count + 1)]
    spare, given = total - most - (count - 1), [1] * (count - 1)
    while spare > 0:
        candidates = [i for i in range(count - 1) if given[i] < most]
        pool, remaining = sum([portions[i] for i in candidates]), spare
        for i in candidates:
            more = min(most - given[i], max(1, remaining * portions[i] // pool), spare)
            given[i] = given[i] + more
            spare = spare - more
    return np.array([most] + given)


def uneven(own_key, count, total, limit, lean):
    if count == 2:
        one = jax.random.randint(own_key, (), max(1, total - limit), min(limit, total - 1) + 1)
        return jnp.stack([one, total - one])
    sizes = jnp.asarray(split_up(count, total, limit, lean), jnp.int32)
    pairs = (count - 1) // 2
    giver, sink = sizes[1:1 + 2 * pairs:2], sizes[2:2 + 2 * pairs:2]
    slack = jnp.minimum(giver - 1, limit - sink)
    moved = jax.random.randint(jax.random.fold_in(own_key, 1), (pairs,), 0, 1 << 20) % (slack + 1)
    sizes = sizes.at[1:1 + 2 * pairs:2].set(giver - moved).at[2:2 + 2 * pairs:2].set(sink + moved)
    return sizes[jax.random.permutation(jax.random.fold_in(own_key, 2), count)]


def scatter_about(rng, dims, deviation, bound, cuts=(), held_as=jnp.bfloat16):
    entries = deviation * jax.random.normal(rng, dims, jnp.float32)
    if cuts:
        entries = entries * levels(rng, dims, cuts, -0.22, 0.18)
    return jnp.clip(entries, -bound, bound).astype(held_as)


def setup_inputs(seed: int = 0, part: int = 0) -> dict:
    splits = jax.random.split(jax.random.key(seed), 8)
    part_splits = jax.random.split(jax.random.fold_in(splits[7], part), 8)
    queries = draw_queries(jax.random.fold_in(jax.random.fold_in(splits[7], part), 71), part)
    prompt_keys = draw_prompt_keys(jax.random.fold_in(jax.random.fold_in(splits[7], part), 71), part)
    prompt_values = scatter_about(part_splits[2], (PROMPT, KVH * HD), 1.0, 6.0, ((0, 16),))
    suffix_keys = draw_suffix_keys(jax.random.fold_in(jax.random.fold_in(splits[7], part), 71), part)
    suffix_values = scatter_about(part_splits[4], (SAMPLES, PAGES, PAGE, KVH * HD), 1.0, 6.0, ((0, 16),))
    suffix_lengths = uneven(part_splits[5], SAMPLES, SAMPLES * SUF_MAX * 5 // 8, SUF_MAX, 2).astype(jnp.int32)
    block_tables = jax.vmap(lambda own: jax.random.permutation(own, PAGES))(jax.random.split(part_splits[6], SAMPLES)).reshape((SAMPLES, PAGES)).astype(jnp.int32)
    return {"queries": queries, "prompt_keys": prompt_keys, "prompt_values": prompt_values, "suffix_keys": suffix_keys, "suffix_values": suffix_values, "suffix_lengths": suffix_lengths, "block_tables": block_tables}


def prompt_partial(query_heads, key_block, value_block):
    scores = jnp.einsum('skgd,pkd->skgp', query_heads.astype(jnp.float32), key_block.astype(jnp.float32)) * (1.0 / math.sqrt(HD))
    maxima = lax.optimization_barrier(jnp.max(scores, axis=-1))
    expos = jnp.exp(scores - maxima[..., None])
    totals = lax.optimization_barrier(jnp.sum(expos, axis=-1))
    weights = lax.optimization_barrier(expos.astype(jnp.bfloat16))
    numerators = jnp.einsum('skgp,pkd->skgd', weights.astype(jnp.float32), value_block.astype(jnp.float32))
    return (maxima, totals, numerators)

def suffix_partial(query_heads, key_pages, value_pages, live_mask):
    scores = jnp.einsum('skgd,stkd->skgt', query_heads.astype(jnp.float32), key_pages.astype(jnp.float32)) * (1.0 / math.sqrt(HD))
    scores = jnp.where(live_mask[:, None, None, :], scores, -jnp.inf)
    maxima = lax.optimization_barrier(jnp.max(scores, axis=-1))
    expos = jnp.exp(scores - maxima[..., None])
    totals = lax.optimization_barrier(jnp.sum(expos, axis=-1))
    weights = lax.optimization_barrier(expos.astype(jnp.bfloat16))
    numerators = jnp.einsum('skgt,stkd->skgd', weights.astype(jnp.float32), value_pages.astype(jnp.float32))
    return (maxima, totals, numerators)

def reference(queries, prompt_keys, prompt_values, suffix_keys, suffix_values, suffix_lengths, block_tables):
    samples = queries.shape[0]
    per_kv = H // KVH
    query_heads = queries.reshape(samples, KVH, per_kv, HD)
    key_shards = prompt_keys.reshape(N_SEQ, PROMPT_DEV, KVH, HD)
    value_shards = prompt_values.reshape(N_SEQ, PROMPT_DEV, KVH, HD)

    def absorb(carry, shard):
        run_max, run_total, run_num = carry
        maxima, totals, numerators = prompt_partial(query_heads, shard[0], shard[1])
        new_max = jnp.maximum(run_max, maxima)
        old_scale = jnp.exp(run_max - new_max)
        new_scale = jnp.exp(maxima - new_max)
        run_total = run_total * old_scale + totals * new_scale
        run_num = run_num * old_scale[..., None] + numerators * new_scale[..., None]
        return ((new_max, run_total, run_num), None)
    start = (jnp.full((samples, KVH, per_kv), -jnp.inf, jnp.float32), jnp.zeros((samples, KVH, per_kv), jnp.float32), jnp.zeros((samples, KVH, per_kv, HD), jnp.float32))
    carried, _ = lax.scan(absorb, start, (key_shards, value_shards))
    prompt_max, prompt_total, prompt_num = carried
    picker = block_tables.astype(jnp.int32)[:, :, None, None]
    key_pages = jnp.take_along_axis(suffix_keys, picker, axis=1).reshape(samples, PAGES * PAGE, KVH, HD)
    value_pages = jnp.take_along_axis(suffix_values, picker, axis=1).reshape(samples, PAGES * PAGE, KVH, HD)
    live_mask = jnp.arange(PAGES * PAGE, dtype=jnp.int32)[None, :] < suffix_lengths.astype(jnp.int32)[:, None]
    suffix_max, suffix_total, suffix_num = suffix_partial(query_heads, key_pages, value_pages, live_mask)
    overall = jnp.maximum(prompt_max, suffix_max)
    prompt_scale = jnp.exp(prompt_max - overall)
    suffix_scale = jnp.exp(suffix_max - overall)
    numer_sum = prompt_num * prompt_scale[..., None] + suffix_num * suffix_scale[..., None]
    denom_sum = prompt_total * prompt_scale + suffix_total * suffix_scale
    attended = numer_sum / denom_sum[..., None]
    return attended.reshape(samples, H * HD).astype(jnp.bfloat16)
```

```python
import functools
import math

import jax
import jax.numpy as jnp
from jax import lax
from jax.experimental import pallas as pl
from jax.experimental.pallas import tpu as pltpu
from jax.sharding import PartitionSpec as P

H = 128
KVH = 8
HD = 128
G = H // KVH
HALF = H // 2
HK = KVH // 2
LINK = jnp.int16
FULL = 32767.0
LOG2 = math.log2(math.e) / math.sqrt(HD)
NT = (((1,), (1,)), ((), ()))


def kernel(
    n, lens, tables, q, k, v, sk, sv, out,
    qbuf, kbuf, vbuf, skb, svb, osend, orecv, ssend, srecv, osuf, lsuf,
    q_send, q_recv, o_send, o_recv, s_send, s_recv, kv_send, kv_recv, own_sem,
):
    me = lax.axis_index("seq")
    core = lax.rem(me, 2)
    partner = me + 1 - 2 * core
    rows = k.shape[0]
    width = k.shape[1] // 2
    nb = n // 4
    mine = me // 4

    def remote(src, dst, send, recv, peer):
        return pltpu.make_async_remote_copy(
            src_ref=src, dst_ref=dst, send_sem=send, recv_sem=recv,
            device_id={"seq": peer}, device_id_type=pl.DeviceIdType.MESH,
        )

    own_cols = pl.ds(pl.multiple_of(core * width, width), width)
    own_half = pl.ds(pl.multiple_of(core * HALF, HALF), HALF)
    local = [
        pltpu.make_async_copy(sk.at[0], skb, own_sem.at[0]),
        pltpu.make_async_copy(sv.at[0], svb, own_sem.at[1]),
        pltpu.make_async_copy(k.at[:, own_cols], kbuf.at[pl.ds(0, rows)], own_sem.at[2]),
        pltpu.make_async_copy(v.at[:, own_cols], vbuf.at[pl.ds(0, rows)], own_sem.at[3]),
        pltpu.make_async_copy(q.at[own_half], qbuf.at[me], own_sem.at[4]),
    ]
    for copy in local:
        copy.start()

    barrier = pltpu.get_barrier_semaphore()

    @pl.loop(1, n)
    def _(step):
        pl.semaphore_signal(
            barrier, inc=1, device_id={"seq": lax.rem(me + step, n)},
            device_id_type=pl.DeviceIdType.MESH,
        )

    pl.semaphore_wait(barrier, n - 1)

    def peer_of(i):
        group = lax.rem(mine + nb - i // 4, nb)
        return group * 4 + lax.rem(me + i, 4)

    def q_copy(peer):
        cut = pl.ds(pl.multiple_of(lax.rem(peer, 2) * HALF, HALF), HALF)
        return remote(q.at[cut], qbuf.at[me], q_send.at[peer], q_recv.at[me], peer)

    @pl.loop(1, n)
    def _(i):
        q_copy(peer_of(i)).start()

    away_cols = pl.ds(pl.multiple_of((1 - core) * width, width), width)
    kv = [
        remote(k.at[:, away_cols], kbuf.at[pl.ds(rows, rows)], kv_send.at[0], kv_recv.at[0], partner),
        remote(v.at[:, away_cols], vbuf.at[pl.ds(rows, rows)], kv_send.at[1], kv_recv.at[1], partner),
    ]
    for copy in kv:
        copy.start()

    pages, page = skb.shape[0], skb.shape[1]
    slots = pages * page
    lane = lax.broadcasted_iota(jnp.int32, (1, slots), 1)
    at_page = lane // page
    position = lane - at_page * page
    for j in range(pages):
        position = position + jnp.where(at_page == tables[0, j], j * page, 0)
    live = position < lens[0]
    for copy in local[:2]:
        copy.wait()
    for h in range(KVH):
        cols = pl.ds(h * HD, HD)
        keys = skb[:, :, cols].reshape(slots, HD)
        values = svb[:, :, cols].reshape(slots, HD)
        part = pl.ds(h * G, G)
        scores = lax.dot_general(q[part], keys, NT, preferred_element_type=jnp.float32)
        scores = jnp.where(live, scores, -jnp.inf)
        top = jnp.max(scores, axis=1, keepdims=True)
        expos = jnp.exp2((scores - top) * LOG2)
        total = jnp.sum(expos, axis=1, keepdims=True)
        num = jnp.dot(expos.astype(jnp.bfloat16), values, preferred_element_type=jnp.float32)
        osuf[part] = num / total
        lsuf[part] = jnp.broadcast_to(top * LOG2 + jnp.log2(total), (G, HD))

    for copy in local[2:]:
        copy.wait()
    for copy in kv:
        copy.wait_recv()

    def o_copy(peer):
        return remote(osend.at[peer], orecv.at[me], o_send.at[peer], o_recv.at[me], peer)

    def s_copy(peer):
        return remote(ssend.at[peer], srecv.at[me], s_send.at[peer], s_recv.at[me], peer)

    wide = lax.broadcasted_iota(jnp.int32, (G, HD), 1)

    def spread(column):
        tile = jnp.zeros((G, HD), jnp.float32)
        for s in range(4):
            tile = jnp.where(wide == s, column[s * G:(s + 1) * G], tile)
        return tile

    def batch(b, first):
        group = lax.rem(mine + b, nb)
        for j in range(1 if first else 0, 4):
            source = group * 4 + lax.rem(me + j, 4)
            remote(qbuf.at[source], qbuf.at[source], q_send.at[source], q_recv.at[source], partner).wait_recv()
        four = pl.ds(pl.multiple_of(group * 4, 4), 4)
        lses, steps = [], []
        for h in range(HK):
            cols = pl.ds(h * HD, HD)
            asked = qbuf[four, pl.ds(h * G, G), :].reshape(4 * G, HD)
            scores = lax.dot_general(asked, kbuf[:, cols], NT, preferred_element_type=jnp.float32)
            top = jnp.max(scores, axis=1, keepdims=True)
            expos = jnp.exp2((scores - top) * LOG2)
            total = jnp.sum(expos, axis=1, keepdims=True)
            num = jnp.dot(expos.astype(jnp.bfloat16), vbuf[:, cols], preferred_element_type=jnp.float32)
            peak = jnp.maximum(jnp.max(jnp.abs(num), axis=1, keepdims=True), 1e-30)
            fixed = jnp.round(num * (FULL / peak)).astype(jnp.int32).astype(LINK)
            osend[four, pl.ds(h * G, G), :] = fixed.reshape(4, G, HD)
            lses.append(spread(top * LOG2 + jnp.log2(total)))
            steps.append(spread(peak / (FULL * total)))
        flat = jnp.concatenate(lses + steps, axis=0).T
        for s in range(4):
            ssend[group * 4 + s] = flat[s:s + 1]
        for j in range(1 if first else 0, 4):
            peer = group * 4 + lax.rem(me + j, 4)
            o_copy(peer).start()
            s_copy(peer).start()
        if first:
            pltpu.make_async_copy(osend.at[me], orecv.at[me], own_sem.at[5]).start()
            pltpu.make_async_copy(ssend.at[me], srecv.at[me], own_sem.at[6]).start()

    batch(0, True)

    @pl.loop(1, nb)
    def _(b):
        batch(b, False)

    pltpu.make_async_copy(osend.at[me], orecv.at[me], own_sem.at[5]).wait()
    pltpu.make_async_copy(ssend.at[me], srecv.at[me], own_sem.at[6]).wait()

    @pl.loop(1, n)
    def _(i):
        source = lax.rem(me + i, n)
        s_copy(source).wait_send()
        remote(ssend.at[source], srecv.at[source], s_send.at[source], s_recv.at[source], partner).wait_recv()

    flat = srecv[...].reshape(n, HD)
    if n % HD:
        flat = jnp.concatenate([flat, jnp.zeros((HD - n % HD, HD), jnp.float32)], axis=0)
    turned = flat.T
    lse, steps = turned[:HALF], turned[HALF:]
    from_lane = lax.broadcasted_iota(jnp.int32, lse.shape, 1)

    @pl.loop(1, n)
    def _(i):
        source = lax.rem(me + i, n)
        o_copy(source).wait_send()
        remote(osend.at[source], orecv.at[source], o_send.at[source], o_recv.at[source], partner).wait_recv()

    for half in range(2):
        part = pl.ds(half * HALF, HALF)
        ok = jnp.logical_and(lax.rem(from_lane, 2) == half, from_lane < n)
        there = jnp.where(ok, lse, -jnp.inf)
        suffix = lsuf[part]
        top = jnp.maximum(jnp.max(there, axis=1, keepdims=True), suffix[:, :1])
        weight = jnp.exp2(there - top)
        own = jnp.exp2(suffix[:, :1] - top)
        total = jnp.sum(weight, axis=1, keepdims=True) + own
        weight = weight * jnp.where(ok, steps, 0.0)
        acc = osuf[part] * own
        for chip in range(n // 2):
            source = 2 * chip + half
            acc = acc + weight[:, source:source + 1] * orecv[source].astype(jnp.float32)
        out[part] = (acc / total).astype(jnp.bfloat16)

    for copy in kv:
        copy.wait_send()

    @pl.loop(1, n)
    def _(i):
        q_copy(peer_of(i)).wait_send()


def per_device(n, queries, keys, values, suffix_keys, suffix_values, lengths, tables):
    rows = keys.shape[0]
    pages, page, width = suffix_keys.shape[1:]
    dma = pltpu.SemaphoreType.DMA
    anywhere = pl.BlockSpec(memory_space=pl.ANY)
    scalar = pl.BlockSpec(memory_space=pltpu.SMEM)
    vector = pl.BlockSpec(memory_space=pltpu.VMEM)
    out = pl.pallas_call(
        functools.partial(kernel, n),
        out_shape=jax.ShapeDtypeStruct((H, HD), jnp.bfloat16),
        in_specs=[scalar, scalar, vector, anywhere, anywhere, anywhere, anywhere],
        out_specs=vector,
        scratch_shapes=[
            pltpu.VMEM((n, HALF, HD), jnp.bfloat16),
            pltpu.VMEM((2 * rows, width // 2), jnp.bfloat16),
            pltpu.VMEM((2 * rows, width // 2), jnp.bfloat16),
            pltpu.VMEM((pages, page, width), jnp.bfloat16),
            pltpu.VMEM((pages, page, width), jnp.bfloat16),
            pltpu.VMEM((n, HALF, HD), LINK),
            pltpu.VMEM((n, HALF, HD), LINK),
            pltpu.VMEM((n, 1, HD), jnp.float32),
            pltpu.VMEM((n, 1, HD), jnp.float32),
            pltpu.VMEM((H, HD), jnp.float32),
            pltpu.VMEM((H, HD), jnp.float32),
            dma((n,)), dma((n,)), dma((n,)), dma((n,)), dma((n,)), dma((n,)),
            dma((2,)), dma((2,)), dma((7,)),
        ],
        compiler_params=pltpu.CompilerParams(collective_id=0, has_side_effects=True),
        name="attend",
    )(lengths, tables, queries.reshape(H, HD), keys, values, suffix_keys, suffix_values)
    return out.reshape(1, H * HD)


def solution(mesh):
    rows = P(("groups", "seq"), None)
    pages = P(("groups", "seq"), None, None, None)
    return jax.shard_map(
        functools.partial(per_device, mesh.shape["seq"]),
        mesh=mesh,
        in_specs=(rows, rows, rows, pages, pages, P(("groups", "seq")), rows),
        out_specs=rows,
        check_vma=False,
    )
```

```python
import functools
import math

import jax
import jax.numpy as jnp
from jax import lax
from jax.experimental import pallas as pl
from jax.experimental.pallas import tpu as pltpu
from jax.sharding import PartitionSpec as P

H = 128
KVH = 8
HD = 128
G = H // KVH
HALF = H // 2
HK = KVH // 2
LINK = jnp.int16
UNROLL = 16
FULL = 32767.0
LOG2 = math.log2(math.e) / math.sqrt(HD)
NT = (((1,), (1,)), ((), ()))


def kernel(
    n, lens, tables, flat_q, k, v, sk, sv, out,
    q, rows32, qbuf, kbuf, vbuf, skb, svb, osend, orecv, ssend, srecv, osuf, lsuf,
    q_send, q_recv, o_send, o_recv, s_send, s_recv, kv_send, kv_recv, own_sem,
):
    me = lax.axis_index("seq")
    core = lax.rem(me, 2)
    partner = me + 1 - 2 * core
    rows = k.shape[0]
    width = k.shape[1] // 2
    nb = n // 4
    mine = me // 4

    def remote(src, dst, send, recv, peer):
        return pltpu.make_async_remote_copy(
            src_ref=src, dst_ref=dst, send_sem=send, recv_sem=recv,
            device_id={"seq": peer}, device_id_type=pl.DeviceIdType.MESH,
        )

    own_cols = pl.ds(pl.multiple_of(core * width, width), width)
    own_half = pl.ds(pl.multiple_of(core * HALF, HALF), HALF)
    local = [
        pltpu.make_async_copy(sk.at[0], skb, own_sem.at[0]),
        pltpu.make_async_copy(sv.at[0], svb, own_sem.at[1]),
        pltpu.make_async_copy(k.at[:, own_cols], kbuf.at[pl.ds(0, rows)], own_sem.at[2]),
        pltpu.make_async_copy(v.at[:, own_cols], vbuf.at[pl.ds(0, rows)], own_sem.at[3]),
    ]
    for copy in local:
        copy.start()

    barrier = pltpu.get_barrier_semaphore()

    def each(low, high, step):
        if n <= UNROLL:
            for i in range(low, high):
                step(i)
        else:
            pl.loop(low, high)(step)

    def peer_of(i):
        group = lax.rem(mine + nb - i // 4, nb)
        return group * 4 + lax.rem(me + i, 4)

    def greet(i):
        pl.semaphore_signal(
            barrier, inc=1, device_id={"seq": peer_of(n - i)},
            device_id_type=pl.DeviceIdType.MESH,
        )

    each(1, n, greet)
    for h in range(H):
        rows32[h:h + 1] = flat_q[:, h * HD:(h + 1) * HD].astype(jnp.float32)
    q[...] = rows32[...].astype(jnp.bfloat16)
    qbuf[me] = q[own_half]
    pl.semaphore_wait(barrier, n - 1)

    def q_copy(peer):
        cut = pl.ds(pl.multiple_of(lax.rem(peer, 2) * HALF, HALF), HALF)
        return remote(q.at[cut], qbuf.at[me], q_send.at[peer], q_recv.at[me], peer)

    each(1, n, lambda i: q_copy(peer_of(i)).start())

    away_cols = pl.ds(pl.multiple_of((1 - core) * width, width), width)
    kv = [
        remote(k.at[:, away_cols], kbuf.at[pl.ds(rows, rows)], kv_send.at[0], kv_recv.at[0], partner),
        remote(v.at[:, away_cols], vbuf.at[pl.ds(rows, rows)], kv_send.at[1], kv_recv.at[1], partner),
    ]
    for copy in kv:
        copy.start()

    pages, page = skb.shape[0], skb.shape[1]
    slots = pages * page
    lane = lax.broadcasted_iota(jnp.int32, (1, slots), 1)
    at_page = lane // page
    position = lane - at_page * page
    for j in range(pages):
        position = position + jnp.where(at_page == tables[0, j], j * page, 0)
    live = position < lens[0]
    for copy in local[:2]:
        copy.wait()
    for h in range(KVH):
        cols = pl.ds(h * HD, HD)
        keys = skb[:, :, cols].reshape(slots, HD)
        values = svb[:, :, cols].reshape(slots, HD)
        part = pl.ds(h * G, G)
        scores = lax.dot_general(q[part], keys, NT, preferred_element_type=jnp.float32)
        scores = jnp.where(live, scores, -jnp.inf)
        top = jnp.max(scores, axis=1, keepdims=True)
        expos = jnp.exp2((scores - top) * LOG2)
        total = jnp.sum(expos, axis=1, keepdims=True)
        num = jnp.dot(expos.astype(jnp.bfloat16), values, preferred_element_type=jnp.float32)
        osuf[part] = num / total
        lsuf[part] = jnp.broadcast_to(top * LOG2 + jnp.log2(total), (G, HD))

    for copy in local[2:]:
        copy.wait()
    for copy in kv:
        copy.wait_recv()

    def o_copy(peer):
        return remote(osend.at[peer], orecv.at[me], o_send.at[peer], o_recv.at[me], peer)

    def s_copy(peer):
        return remote(ssend.at[peer], srecv.at[me], s_send.at[peer], s_recv.at[me], peer)

    wide = lax.broadcasted_iota(jnp.int32, (G, HD), 1)

    def spread(column):
        tile = jnp.zeros((G, HD), jnp.float32)
        for s in range(4):
            tile = jnp.where(wide == s, column[s * G:(s + 1) * G], tile)
        return tile

    def batch(b, first):
        group = lax.rem(mine + b, nb)
        for j in range(1 if first else 0, 4):
            source = group * 4 + lax.rem(me + j, 4)
            remote(qbuf.at[source], qbuf.at[source], q_send.at[source], q_recv.at[source], partner).wait_recv()
        four = pl.ds(pl.multiple_of(group * 4, 4), 4)
        lses, steps = [], []
        ones = jnp.ones((kbuf.shape[0], HD), jnp.bfloat16)
        for h in range(HK):
            cols = pl.ds(h * HD, HD)
            asked = qbuf[four, pl.ds(h * G, G), :].reshape(4 * G, HD)
            scores = lax.dot_general(asked, kbuf[:, cols], NT, preferred_element_type=jnp.float32)
            top = jnp.max(scores, axis=1, keepdims=True)
            expos = jnp.exp2((scores - top) * LOG2)
            wider = jnp.concatenate([vbuf[:, cols], ones], axis=1)
            both = jnp.dot(expos.astype(jnp.bfloat16), wider, preferred_element_type=jnp.float32)
            num, total = both[:, :HD], both[:, HD:]
            peak = jnp.maximum(jnp.max(jnp.abs(num), axis=1, keepdims=True), 1e-30)
            fixed = jnp.round(num * (FULL / peak)).astype(jnp.int32).astype(LINK)
            osend[four, pl.ds(h * G, G), :] = fixed.reshape(4, G, HD)
            lses.append(spread(top * LOG2 + jnp.log2(total)))
            steps.append(spread(peak / (FULL * total)))
        flat = jnp.concatenate(lses + steps, axis=0).T
        for s in range(4):
            ssend[group * 4 + s] = flat[s:s + 1]
        for j in range(1 if first else 0, 4):
            peer = group * 4 + lax.rem(me + j, 4)
            o_copy(peer).start()
            s_copy(peer).start()
        if first:
            pltpu.make_async_copy(osend.at[me], orecv.at[me], own_sem.at[5]).start()
            pltpu.make_async_copy(ssend.at[me], srecv.at[me], own_sem.at[6]).start()

    batch(0, True)

    each(1, nb, lambda b: batch(b, False))

    order = [lax.rem(mine + i // 4, nb) * 4 + lax.rem(me + i, 4) for i in range(n)]
    pltpu.make_async_copy(ssend.at[me], srecv.at[me], own_sem.at[6]).wait()
    for source in order[1:]:
        remote(ssend.at[source], srecv.at[source], s_send.at[source], s_recv.at[source], partner).wait_recv()
    flat = [srecv[source] for source in order]
    if n % HD:
        flat.append(jnp.zeros((HD - n % HD, HD), jnp.float32))
    turned = jnp.concatenate(flat, axis=0).T
    lse, steps = turned[:HALF], turned[HALF:]
    from_lane = lax.broadcasted_iota(jnp.int32, lse.shape, 1)
    accs, weights, totals, parts = [], [], [], []
    for side in range(2):
        half = lax.rem(core + side, 2)
        part = pl.ds(pl.multiple_of(half * HALF, HALF), HALF)
        ok = jnp.logical_and(lax.rem(from_lane, 2) == side, from_lane < n)
        there = jnp.where(ok, lse, -jnp.inf)
        suffix = lsuf[part]
        top = jnp.maximum(jnp.max(there, axis=1, keepdims=True), suffix[:, :1])
        weight = jnp.exp2(there - top)
        own = jnp.exp2(suffix[:, :1] - top)
        total = jnp.sum(weight, axis=1, keepdims=True) + own
        inverse = 1.0 / total
        weights.append(weight * jnp.where(ok, steps, 0.0) * inverse)
        accs.append(osuf[part] * (own * inverse))
    pltpu.make_async_copy(osend.at[me], orecv.at[me], own_sem.at[5]).wait()
    for i, source in enumerate(order):
        if i:
            remote(osend.at[source], orecv.at[source], o_send.at[source], o_recv.at[source], partner).wait_recv()
        side = i % 2
        accs[side] = accs[side] + weights[side][:, i:i + 1] * orecv[source].astype(jnp.float32)
    for side in range(2):
        base = lax.rem(core + side, 2) * HALF
        done = accs[side]
        for h in range(HALF):
            at = pl.ds(pl.multiple_of((base + h) * HD, HD), HD)
            out[:, at] = done[h:h + 1].astype(jnp.bfloat16)

    for copy in kv:
        copy.wait_send()

    def left(i):
        peer = peer_of(i)
        q_copy(peer).wait_send()
        o_copy(peer).wait_send()
        s_copy(peer).wait_send()

    each(1, n, left)


def per_device(n, queries, keys, values, suffix_keys, suffix_values, lengths, tables):
    rows = keys.shape[0]
    pages, page, width = suffix_keys.shape[1:]
    dma = pltpu.SemaphoreType.DMA
    anywhere = pl.BlockSpec(memory_space=pl.ANY)
    scalar = pl.BlockSpec(memory_space=pltpu.SMEM)
    vector = pl.BlockSpec(memory_space=pltpu.VMEM)
    out = pl.pallas_call(
        functools.partial(kernel, n),
        out_shape=jax.ShapeDtypeStruct((1, H * HD), jnp.bfloat16),
        in_specs=[scalar, scalar, vector, anywhere, anywhere, anywhere, anywhere],
        out_specs=vector,
        scratch_shapes=[
            pltpu.VMEM((H, HD), jnp.bfloat16),
            pltpu.VMEM((H, HD), jnp.float32),
            pltpu.VMEM((n, HALF, HD), jnp.bfloat16),
            pltpu.VMEM((2 * rows, width // 2), jnp.bfloat16),
            pltpu.VMEM((2 * rows, width // 2), jnp.bfloat16),
            pltpu.VMEM((pages, page, width), jnp.bfloat16),
            pltpu.VMEM((pages, page, width), jnp.bfloat16),
            pltpu.VMEM((n, HALF, HD), LINK),
            pltpu.VMEM((n, HALF, HD), LINK),
            pltpu.VMEM((n, 1, HD), jnp.float32),
            pltpu.VMEM((n, 1, HD), jnp.float32),
            pltpu.VMEM((H, HD), jnp.float32),
            pltpu.VMEM((H, HD), jnp.float32),
            dma((n,)), dma((n,)), dma((n,)), dma((n,)), dma((n,)), dma((n,)),
            dma((2,)), dma((2,)), dma((7,)),
        ],
        compiler_params=pltpu.CompilerParams(collective_id=0, has_side_effects=True),
        name="attend",
    )(lengths, tables, queries, keys, values, suffix_keys, suffix_values)
    return out


def solution(mesh):
    rows = P(("groups", "seq"), None)
    pages = P(("groups", "seq"), None, None, None)
    return jax.shard_map(
        functools.partial(per_device, mesh.shape["seq"]),
        mesh=mesh,
        in_specs=(rows, rows, rows, pages, pages, P(("groups", "seq")), rows),
        out_specs=rows,
        check_vma=False,
    )
```

```python
import functools
import math

import jax
import jax.numpy as jnp
from jax import lax
from jax.experimental import pallas as pl
from jax.experimental.pallas import tpu as pltpu
from jax.sharding import PartitionSpec as P

H = 128
KVH = 8
HD = 128
G = H // KVH
HALF = H // 2
HK = KVH // 2
LINK = jnp.int16
UNROLL = 16
FULL = 32767.0
SCALE = 1.0 / math.sqrt(HD)
NT = (((1,), (1,)), ((), ()))


def kernel(
    n, lens, tables, flat_q, k, v, sk, sv, out,
    q, rows32, qbuf, kbuf, vbuf, skb, svb, osend, orecv, ssend, srecv, osuf, lsuf,
    q_send, q_recv, o_send, o_recv, s_send, s_recv, kv_send, kv_recv, own_sem,
):
    me = lax.axis_index("seq")
    core = lax.rem(me, 2)
    partner = me + 1 - 2 * core
    rows = k.shape[0]
    width = k.shape[1] // 2
    nb = n // 4
    mine = me // 4

    def remote(src, dst, send, recv, peer):
        return pltpu.make_async_remote_copy(
            src_ref=src, dst_ref=dst, send_sem=send, recv_sem=recv,
            device_id={"seq": peer}, device_id_type=pl.DeviceIdType.MESH,
        )

    own_cols = pl.ds(pl.multiple_of(core * width, width), width)
    own_half = pl.ds(pl.multiple_of(core * HALF, HALF), HALF)
    local = [
        pltpu.make_async_copy(sk.at[0], skb, own_sem.at[0]),
        pltpu.make_async_copy(sv.at[0], svb, own_sem.at[1]),
        pltpu.make_async_copy(k.at[:, own_cols], kbuf.at[pl.ds(0, rows)], own_sem.at[2]),
        pltpu.make_async_copy(v.at[:, own_cols], vbuf.at[pl.ds(0, rows)], own_sem.at[3]),
    ]
    for copy in local:
        copy.start()

    barrier = pltpu.get_barrier_semaphore()

    def each(low, high, step):
        if n <= UNROLL:
            for i in range(low, high):
                step(i)
        else:
            pl.loop(low, high)(step)

    def peer_of(i):
        group = lax.rem(mine + nb - i // 4, nb)
        return group * 4 + lax.rem(me + i, 4)

    def greet(i):
        pl.semaphore_signal(
            barrier, inc=1, device_id={"seq": peer_of(n - i)},
            device_id_type=pl.DeviceIdType.MESH,
        )

    each(1, n, greet)
    for h in range(H):
        rows32[h:h + 1] = flat_q[:, h * HD:(h + 1) * HD].astype(jnp.float32)
    q[...] = rows32[...].astype(jnp.bfloat16)
    qbuf[me] = q[own_half]
    pages, page = skb.shape[0], skb.shape[1]
    slots = pages * page
    lane = lax.broadcasted_iota(jnp.int32, (1, slots), 1)
    at_page = lane // page
    position = lane - at_page * page
    for j in range(pages):
        position = position + jnp.where(at_page == tables[0, j], j * page, 0)
    live = position < lens[0]
    for copy in local[:2]:
        copy.wait()
    for h in range(KVH):
        cols = pl.ds(h * HD, HD)
        keys = skb[:, :, cols].reshape(slots, HD)
        values = svb[:, :, cols].reshape(slots, HD)
        part = pl.ds(h * G, G)
        scores = lax.dot_general(q[part], keys, NT, preferred_element_type=jnp.float32)
        scores = jnp.where(live, scores, -jnp.inf)
        top = jnp.max(scores, axis=1, keepdims=True)
        expos = jnp.exp((scores - top) * SCALE)
        total = jnp.sum(expos, axis=1, keepdims=True)
        num = jnp.dot(expos.astype(jnp.bfloat16), values, preferred_element_type=jnp.float32)
        osuf[part] = num / total
        lsuf[part] = jnp.broadcast_to(top * SCALE + jnp.log(total), (G, HD))

    pl.semaphore_wait(barrier, n - 1)

    def q_copy(peer):
        cut = pl.ds(pl.multiple_of(lax.rem(peer, 2) * HALF, HALF), HALF)
        return remote(q.at[cut], qbuf.at[me], q_send.at[peer], q_recv.at[me], peer)

    each(4, n, lambda i: q_copy(peer_of(i)).start())
    each(1, 4, lambda i: q_copy(peer_of(i)).start())

    away_cols = pl.ds(pl.multiple_of((1 - core) * width, width), width)
    kv = [
        remote(k.at[:, away_cols], kbuf.at[pl.ds(rows, rows)], kv_send.at[0], kv_recv.at[0], partner),
        remote(v.at[:, away_cols], vbuf.at[pl.ds(rows, rows)], kv_send.at[1], kv_recv.at[1], partner),
    ]
    for copy in kv:
        copy.start()

    for copy in local[2:]:
        copy.wait()
    for copy in kv:
        copy.wait_recv()

    def o_copy(peer):
        return remote(osend.at[peer], orecv.at[me], o_send.at[peer], o_recv.at[me], peer)

    def s_copy(peer):
        return remote(ssend.at[peer], srecv.at[me], s_send.at[peer], s_recv.at[me], peer)

    wide = lax.broadcasted_iota(jnp.int32, (G, HD), 1)

    def spread(column):
        tile = jnp.zeros((G, HD), jnp.float32)
        for s in range(4):
            tile = jnp.where(wide == s, column[s * G:(s + 1) * G], tile)
        return tile

    def batch(b, first):
        group = lax.rem(mine + b, nb)
        for j in range(1 if first else 0, 4):
            source = group * 4 + lax.rem(me + j, 4)
            remote(qbuf.at[source], qbuf.at[source], q_send.at[source], q_recv.at[source], partner).wait_recv()
        four = pl.ds(pl.multiple_of(group * 4, 4), 4)
        lses, steps = [], []
        ones = jnp.ones((kbuf.shape[0], HD), jnp.bfloat16)
        for h in range(HK):
            cols = pl.ds(h * HD, HD)
            asked = qbuf[four, pl.ds(h * G, G), :].reshape(4 * G, HD)
            scores = lax.dot_general(asked, kbuf[:, cols], NT, preferred_element_type=jnp.float32)
            top = jnp.max(scores, axis=1, keepdims=True)
            expos = jnp.exp((scores - top) * SCALE)
            wider = jnp.concatenate([vbuf[:, cols], ones], axis=1)
            both = jnp.dot(expos.astype(jnp.bfloat16), wider, preferred_element_type=jnp.float32)
            num, total = both[:, :HD], both[:, HD:]
            peak = jnp.maximum(jnp.max(jnp.abs(num), axis=1, keepdims=True), 1e-30)
            fixed = jnp.round(num * (FULL / peak)).astype(jnp.int32).astype(LINK)
            osend[four, pl.ds(h * G, G), :] = fixed.reshape(4, G, HD)
            lses.append(spread(top * SCALE + jnp.log(total)))
            steps.append(spread(peak / (FULL * total)))
        flat = jnp.concatenate(lses + steps, axis=0).T
        for s in range(4):
            ssend[group * 4 + s] = flat[s:s + 1]
        for j in range(1 if first else 0, 4):
            peer = group * 4 + lax.rem(me + j, 4)
            s_copy(peer).start()
            o_copy(peer).start()
        if first:
            pltpu.make_async_copy(osend.at[me], orecv.at[me], own_sem.at[5]).start()
            pltpu.make_async_copy(ssend.at[me], srecv.at[me], own_sem.at[6]).start()

    batch(0, True)

    each(1, nb, lambda b: batch(b, False))

    order = [lax.rem(mine + i // 4, nb) * 4 + lax.rem(me + i, 4) for i in range(n)]
    pltpu.make_async_copy(ssend.at[me], srecv.at[me], own_sem.at[6]).wait()
    for source in order[1:]:
        remote(ssend.at[source], srecv.at[source], s_send.at[source], s_recv.at[source], partner).wait_recv()
    flat = [srecv[source] for source in order]
    if n % HD:
        flat.append(jnp.zeros((HD - n % HD, HD), jnp.float32))
    turned = jnp.concatenate(flat, axis=0).T
    lse, steps = turned[:HALF], turned[HALF:]
    from_lane = lax.broadcasted_iota(jnp.int32, lse.shape, 1)
    accs, weights, totals, parts = [], [], [], []
    for side in range(2):
        half = lax.rem(core + side, 2)
        part = pl.ds(pl.multiple_of(half * HALF, HALF), HALF)
        ok = jnp.logical_and(lax.rem(from_lane, 2) == side, from_lane < n)
        there = jnp.where(ok, lse, -jnp.inf)
        suffix = lsuf[part]
        top = jnp.maximum(jnp.max(there, axis=1, keepdims=True), suffix[:, :1])
        weight = jnp.exp(there - top)
        own = jnp.exp(suffix[:, :1] - top)
        total = jnp.sum(weight, axis=1, keepdims=True) + own
        inverse = 1.0 / total
        weights.append(weight * jnp.where(ok, steps, 0.0) * inverse)
        accs.append(osuf[part] * (own * inverse))
    pltpu.make_async_copy(osend.at[me], orecv.at[me], own_sem.at[5]).wait()
    for i, source in enumerate(order):
        if i:
            remote(osend.at[source], orecv.at[source], o_send.at[source], o_recv.at[source], partner).wait_recv()
        side = i % 2
        accs[side] = accs[side] + weights[side][:, i:i + 1] * orecv[source].astype(jnp.float32)
    for side in range(2):
        base = lax.rem(core + side, 2) * HALF
        out[pl.ds(pl.multiple_of(base, HALF), HALF)] = accs[side].astype(jnp.bfloat16)

    for copy in kv:
        copy.wait_send()

    def left(i):
        peer = peer_of(i)
        q_copy(peer).wait_send()
        o_copy(peer).wait_send()
        s_copy(peer).wait_send()

    each(1, n, left)


def per_device(n, queries, keys, values, suffix_keys, suffix_values, lengths, tables):
    rows = keys.shape[0]
    pages, page, width = suffix_keys.shape[1:]
    dma = pltpu.SemaphoreType.DMA
    anywhere = pl.BlockSpec(memory_space=pl.ANY)
    scalar = pl.BlockSpec(memory_space=pltpu.SMEM)
    vector = pl.BlockSpec(memory_space=pltpu.VMEM)
    out = pl.pallas_call(
        functools.partial(kernel, n),
        out_shape=jax.ShapeDtypeStruct((H, HD), jnp.bfloat16),
        in_specs=[scalar, scalar, vector, anywhere, anywhere, anywhere, anywhere],
        out_specs=vector,
        scratch_shapes=[
            pltpu.VMEM((H, HD), jnp.bfloat16),
            pltpu.VMEM((H, HD), jnp.float32),
            pltpu.VMEM((n, HALF, HD), jnp.bfloat16),
            pltpu.VMEM((2 * rows, width // 2), jnp.bfloat16),
            pltpu.VMEM((2 * rows, width // 2), jnp.bfloat16),
            pltpu.VMEM((pages, page, width), jnp.bfloat16),
            pltpu.VMEM((pages, page, width), jnp.bfloat16),
            pltpu.VMEM((n, HALF, HD), LINK),
            pltpu.VMEM((n, HALF, HD), LINK),
            pltpu.VMEM((n, 1, HD), jnp.float32),
            pltpu.VMEM((n, 1, HD), jnp.float32),
            pltpu.VMEM((H, HD), jnp.float32),
            pltpu.VMEM((H, HD), jnp.float32),
            dma((n,)), dma((n,)), dma((n,)), dma((n,)), dma((n,)), dma((n,)),
            dma((2,)), dma((2,)), dma((7,)),
        ],
        compiler_params=pltpu.CompilerParams(collective_id=0, has_side_effects=True),
        name="attend",
    )(lengths, tables, queries, keys, values, suffix_keys, suffix_values)
    return out.reshape(1, H * HD)


def solution(mesh):
    rows = P(("groups", "seq"), None)
    pages = P(("groups", "seq"), None, None, None)
    return jax.shard_map(
        functools.partial(per_device, mesh.shape["seq"]),
        mesh=mesh,
        in_specs=(rows, rows, rows, pages, pages, P(("groups", "seq")), rows),
        out_specs=rows,
        check_vma=False,
    )
```
